32 devices in a mesh: district: 4 (over y, core), sub: 8 (over z, x).
Axes of the slice: x: 2, y: 2, z: 4, core: 2. Of those that a mesh axis runs over, the one named last changes fastest.
Arguments:
- cost_terms: bfloat16 [8, 512, 768], P('district', 'sub'), may hold values from -6 to 6
- neighbours: int32 [8, 512, 4], P('district', 'sub'), may hold values from 0 to 511, as said below
- relayout: int32 [8, 512], P('district'), may hold values from 0 to 511, as said below
- ownership: int32 [8, 512], P('district', 'sub'), may hold values from 0 to 31
- capacity: float32 [16, 48], replicated, may hold values from -67.88225 to 67.88225
- coupling: bfloat16 [8, 768, 192], P('district'), may hold values from -0.21875 to 0.21875
- solve_factor: bfloat16 [8, 768, 768], P('district')
Outputs:
- control_plan: float32 [8, 512, 768], P('district', 'sub')
- flow_prices: float32 [8, 512, 192], P('district', 'sub')
- reservoir_duals: float32 [16, 48], replicated
The draws below stay inside these ranges and needn't reach their ends.
Inputs may be any that keep to these rules, and one draw needn't show every extreme that they name: `neighbours`: each entry lies within 16 of its own balanced position and differs from it. `relayout`: each row is a permutation; of the subsystems at geographic positions s * 64 to (s + 1) * 64 - 1, exactly 8 go to balanced positions j * 64 to (j + 1) * 64 - 1, for every s and j. `ownership`: values of 16 or more mean that the subsystem draws from no reservoir.
All inputs are finite; a program needn't handle non-finite values.
Results may differ from the reference program's by a relative error of at most 0.018.
Values may be sent and summed in bfloat16 or wider, within the bound.
No kernel may reach another device: no remote copies, remote signals or barrier semaphores. Data moves between devices by JAX's collectives and lax.ppermute only.
A program may use at most 64 MiB of HBM per device.

```python
import math
import jax
import jax.numpy as jnp
from jax import lax

HORIZON = 48
UNKNOWNS = 768
INTERFACE = 192
SUB_DEV = 64
DISTRICTS = 8
SUB_DIST = 512
PEER_SHARE = 8
REACH_SPAN = 16
LINK_COUNT = 4
RESERVOIRS = 16
RESERVOIR_LOAD = 128
OUTER_ITERS = 2
INNER_ITERS = 4


def draw_neighbours(key, part):
    picks = jax.random.randint(key, (DISTRICTS, SUB_DIST, LINK_COUNT), 0, 2 * REACH_SPAN)
    offsets = picks - REACH_SPAN + (picks >= REACH_SPAN).astype(jnp.int32)
    places = jnp.arange(SUB_DIST, dtype=jnp.int32)[None, :, None]
    target = places + offsets
    target = jnp.where((target < 0) | (target >= SUB_DIST), places - offsets, target)
    return target.astype(jnp.int32)


def draw_relayout(key, part):
    first_key = jax.random.fold_in(key, 11)
    second_key = jax.random.fold_in(key, 23)
    groups = SUB_DIST // SUB_DEV
    base = jnp.tile(jnp.arange(SUB_DEV, dtype=jnp.int32)[None, :], (DISTRICTS * groups, 1))
    source_perm = jax.random.permutation(first_key, base, axis=1, independent=True).reshape(DISTRICTS, groups, SUB_DEV)
    target_perm = jax.random.permutation(second_key, base, axis=1, independent=True).reshape(DISTRICTS, groups, SUB_DEV)
    dest_block = source_perm // PEER_SHARE
    within = source_perm % PEER_SHARE
    sources = jnp.arange(groups, dtype=jnp.int32)[None, :, None]
    slot_index = sources * PEER_SHARE + within
    district_rows = jnp.arange(DISTRICTS, dtype=jnp.int32)[:, None, None]
    target = dest_block * SUB_DEV + target_perm[district_rows, dest_block, slot_index]
    return target.reshape(DISTRICTS, SUB_DIST).astype(jnp.int32)


def draw_solve_factor(key, part):
    first_key = jax.random.fold_in(key, 5)
    second_key = jax.random.fold_in(key, 7)
    diagonal = jnp.exp(jax.random.uniform(first_key, (DISTRICTS, UNKNOWNS), jnp.float32, jnp.log(0.5), jnp.log(2.0)))
    spread = jax.random.normal(second_key, (DISTRICTS, UNKNOWNS, UNKNOWNS), jnp.float32) * (0.5 / UNKNOWNS ** 0.5)
    matrix = spread + diagonal[:, :, None] * jnp.eye(UNKNOWNS, dtype=jnp.float32)[None, :, :]
    return matrix.astype(jnp.bfloat16)


def set_ends(entries, own_key, low, high):
    dims = entries.shape
    index_at = [jax.random.randint(jax.random.fold_in(own_key, axis), (), 0, dims[axis]) for axis in range(len(dims))]
    entries = entries.at[tuple(index_at)].set(low)
    longest = dims.index(max(dims))
    index_at[longest] = (index_at[longest] + 1) % dims[longest]
    return entries.at[tuple(index_at)].set(high)


def shard_levels(key, shape, pieces, least, high):
    factor_of, own = 1.0, jax.random.fold_in(key, 6)
    for position, parts in pieces:
        heights = jnp.exp(jax.random.uniform(jax.random.fold_in(own, position), (parts,), jnp.float32, least / len(pieces), high / len(pieces)))
        factor_of = factor_of * jnp.repeat(heights, shape[position] // parts).reshape([-1 if axis == position else 1 for axis in range(len(shape))])
    return factor_of


def normal_values(stream_key, shape, scale, limit, split=(), held_as=jnp.bfloat16):
    values = scale * jax.random.normal(stream_key, shape, jnp.float32)
    if split:
        values = values * shard_levels(stream_key, shape, split, -0.22, 0.18)
    return jnp.clip(values, -limit, limit).astype(held_as)


def setup_inputs(seed: int = 0) -> dict:
    seeds = jax.random.split(jax.random.key(seed), 8)
    return {
        "cost_terms": normal_values(seeds[0], (DISTRICTS, SUB_DIST, UNKNOWNS), 1.0, 6.0, ((0, 4), (1, 8))),
        "neighbours": draw_neighbours(jax.random.fold_in(seeds[7], 71), 0),
        "relayout": draw_relayout(jax.random.fold_in(seeds[7], 71), 0),
        "ownership": set_ends(jax.random.randint(seeds[3], (DISTRICTS, SUB_DIST), 0, 2 * RESERVOIRS), jax.random.fold_in(seeds[3], 1), 0, (2 * RESERVOIRS) - 1).astype(jnp.int32),
        "capacity": normal_values(seeds[4], (RESERVOIRS, HORIZON), (RESERVOIR_LOAD ** 0.5), 67.88225, (), jnp.float32),
        "coupling": normal_values(seeds[5], (DISTRICTS, UNKNOWNS, INTERFACE), UNKNOWNS ** -0.5, 0.21875, ((0, 4),)),
        "solve_factor": draw_solve_factor(jax.random.fold_in(seeds[7], 71), 0),
    }


price_step = 0.3
reserve_step = 1.0

def neighbour_mean(values, links):
    district_rows = jnp.arange(values.shape[0], dtype=jnp.int32)[:, None]
    running = jnp.zeros(links.shape[:2] + values.shape[2:], jnp.float32)
    for which in range(LINK_COUNT):
        running = running + values[district_rows, links[:, :, which]].astype(jnp.float32)
    return running / LINK_COUNT

def reference(cost_terms, neighbours, relayout, ownership, capacity, coupling, solve_factor):
    district_rows = jnp.arange(DISTRICTS, dtype=jnp.int32)[:, None]
    inverse = jnp.argsort(relayout, axis=1, stable=True).astype(jnp.int32)
    balanced_costs = cost_terms[district_rows, inverse]
    owner_slot = jnp.where(ownership < RESERVOIRS, ownership, RESERVOIRS).astype(jnp.int32)
    flow_prices = jnp.zeros((DISTRICTS, SUB_DIST, INTERFACE), jnp.float32)
    reserve_duals = jnp.zeros((RESERVOIRS, HORIZON), jnp.float32)
    dual_scale = reserve_step / math.sqrt(RESERVOIR_LOAD)
    highest = lax.Precision.HIGHEST
    coupling_wide = coupling.astype(jnp.float32)
    factor_wide = solve_factor.astype(jnp.float32)
    plan_now = None
    flow_now = None
    for outer_step in range(OUTER_ITERS):
        for inner_step in range(INNER_ITERS):
            padded_duals = jnp.concatenate([reserve_duals, jnp.zeros((1, HORIZON), jnp.float32)], axis=0)
            boundary = padded_duals[owner_slot]
            boundary = jnp.concatenate([boundary, jnp.zeros((DISTRICTS, SUB_DIST, INTERFACE - HORIZON), jnp.float32)], axis=2)
            price_term = (flow_prices - neighbour_mean(flow_prices, neighbours) + boundary).astype(jnp.bfloat16)
            gradient = (balanced_costs.astype(jnp.float32) + jnp.einsum('dsf,dzf->dsz', price_term.astype(jnp.float32), coupling_wide, precision=highest)).astype(jnp.bfloat16)
            plan_now = -jnp.einsum('dsz,dzw->dsw', gradient.astype(jnp.float32), factor_wide, precision=highest)
            plan_rounded = plan_now.astype(jnp.bfloat16)
            flow_now = jnp.einsum('dsz,dzf->dsf', plan_rounded.astype(jnp.float32), coupling_wide, precision=highest).astype(jnp.bfloat16)
            flow_prices = flow_prices + price_step * (flow_now.astype(jnp.float32) - neighbour_mean(flow_now, neighbours))
        draws = jax.ops.segment_sum(flow_now[:, :, :HORIZON].astype(jnp.float32).reshape(-1, HORIZON), owner_slot.reshape(-1), num_segments=RESERVOIRS + 1)[:RESERVOIRS]
        reserve_duals = reserve_duals + (draws - capacity) * dual_scale
    control_plan = plan_now[district_rows, relayout]
    return (control_plan, flow_prices, reserve_duals)
```

```python
import functools
import math

import jax
import jax.numpy as jnp
from jax import lax
from jax.experimental import pallas as pl
from jax.experimental.pallas import tpu as pltpu
from jax.sharding import PartitionSpec as P

REACH_SPAN = 16
LINK_COUNT = 4
RESERVOIRS = 16
OUTER_ITERS = 2
INNER_ITERS = 4

PRICE_STEP = 0.3
RESERVE_STEP = 1.0

LANES = 128
PAD = 2 * REACH_SPAN

BF = jnp.bfloat16
F32 = jnp.float32


def mm(a, b):
    return jnp.dot(a, b, preferred_element_type=F32)


def mm_nt(a, b):
    return lax.dot_general(a, b, (((1,), (1,)), ((), ())), preferred_element_type=F32)


def mm_tn(a, b):
    return lax.dot_general(a, b, (((0,), (0,)), ((), ())), preferred_element_type=F32)


def iota(shape, dim):
    return lax.broadcasted_iota(jnp.int32, shape, dim)


def each(count, step):
    if count <= 8:
        for i in range(count):
            step(i)
    else:
        lax.fori_loop(0, count, lambda i, c: (step(i), c)[1], 0)


def at(i, size):
    if isinstance(i, int):
        return pl.ds(i * size, size)
    return pl.ds(pl.multiple_of(i * size, size), size)


def window(i, size, width):
    if isinstance(i, int):
        return pl.ds(i * size, width)
    return pl.ds(pl.multiple_of(i * size, size), width)


def prepare_body(my_ref, cost_ref, s_ref, c_ref, nb_ref, own_ref, y_ref, z_ref, m_ref, pay_ref,
                 lhs, acc, *, rows, width, chunk, owner_at):
    d = pl.program_id(0)
    j = pl.program_id(1)

    @pl.when(j == 0)
    def _():
        lhs[:rows, :] = cost_ref[0]
        lhs[rows:, :] = c_ref[0].T
        acc[...] = jnp.zeros_like(acc)

    yz = mm(lhs[...], s_ref[0])
    y_ref[0] = yz[:rows]
    yzb = yz.astype(BF)
    z_ref[0] = yzb[rows:]
    acc[...] += mm(yzb, c_ref[0, pl.ds(pl.multiple_of(j * chunk, chunk), chunk), :])

    @pl.when(j == pl.num_programs(1) - 1)
    def _():
        pay_ref[0, :, 0:width] = (-acc[:rows]).astype(BF)
        m_ref[0] = acc[rows:].astype(BF)
        total = pay_ref.shape[2]
        own = own_ref[pl.ds(d, 1), :]
        slot = iota((total, rows), 0) - owner_at
        hot = ((slot == own) & (slot >= 0) & (slot < RESERVOIRS)).astype(F32)
        eye = (iota((rows, rows), 0) == iota((rows, rows), 1)).astype(F32)
        ext = mm_nt(eye.astype(BF), hot.astype(BF))
        off = (nb_ref[0] - my_ref[0] * rows - iota((rows, LINK_COUNT), 0)).astype(F32)
        lane = iota((rows, total), 1)
        for k in range(LINK_COUNT):
            ext = jnp.where(lane == width + k, off[:, k:k + 1], ext)
        pay_ref[0, :, width:] = ext[:, width:].astype(BF)


def band(off, rows, columns, shift, first_lane):
    column = iota((rows, columns), 1) - iota((rows, columns), 0) - shift
    out = (column == 0).astype(F32)
    for k in range(LINK_COUNT):
        offset = off[:, first_lane + k:first_lane + k + 1].astype(jnp.int32)
        out = out - jnp.where(column == offset, 1.0 / LINK_COUNT, 0.0)
    return out


def iterate_body(my_ref, g_ref, rel_ref, relown_ref, m_ref,
                 d0_ref, d1_ref, pb_ref, tb_ref, ql_ref, qg_ref, gm_ref, mp_ref,
                 off, dband, x, h, f0, t, exc, fl, *, rows, width, horizon, tile, owner_at):
    districts = g_ref.shape[1]
    subs = g_ref.shape[0]
    total = g_ref.shape[3]
    count = rows * subs
    blocks = count // tile
    low = total - LANES
    span = tile + 2 * PAD
    my = my_ref[0]
    half = iota((tile, LANES), 1)
    own_lane = owner_at - low

    def ext_of(v, power):
        moved = pltpu.roll(v, (power * RESERVOIRS - own_lane) % LANES, 1)
        keep = (half >= power * RESERVOIRS) & (half < (power + 1) * RESERVOIRS)
        return jnp.where(keep, moved, 0.0)

    for d in range(districts):
        off[d, :PAD, :] = jnp.zeros((PAD, LANES), F32)
        off[d, PAD + count:, :] = jnp.zeros((PAD, LANES), F32)
        x[d, :PAD, :] = jnp.zeros((PAD, total), BF)
        x[d, PAD + count:, :] = jnp.zeros((PAD, total), BF)
        exc[d, :PAD, :] = jnp.zeros((PAD, LANES), BF)
        exc[d, PAD + count:, :] = jnp.zeros((PAD, LANES), BF)

        def unpack(s):
            here = at(s, rows)
            if isinstance(s, int):
                padded = pl.ds(PAD + s * rows, rows)
            else:
                padded = pl.ds(pl.multiple_of(PAD + s * rows, PAD), rows)
            block = g_ref[s, d]
            t[d, here, :] = block[:, :width]
            off[d, padded, :] = block[:, low:].astype(F32)
            x[d, padded, :] = block

        each(subs, unpack)

        def order(i):
            place = iota((tile, count), 0) + i * tile
            hot = (place == rel_ref[d:d + 1, :]).astype(F32).astype(BF)
            f0[d, at(i, tile), :] = mm(hot, t[d])

        each(blocks, order)

        def bands(i):
            full = band(off[d, window(i, tile, span), :], span, span, 0, width - low).astype(BF)
            dband[d, at(i, tile), :] = mm(full[PAD:PAD + tile], full).astype(BF)
            if isinstance(i, int):
                padded = pl.ds(PAD + i * tile, tile)
            else:
                padded = pl.ds(pl.multiple_of(PAD + i * tile, PAD), tile)
            f = f0[d, at(i, tile), :]
            h[d, at(i, tile), :] = f
            x[d, padded, :width] = f.astype(BF)
            exc[d, padded, :] = ext_of(off[d, padded, :], 0).astype(BF)

        each(blocks, bands)

    steps = OUTER_ITERS * INNER_ITERS
    for k in range(1, steps):
        for d in range(districts):
            def spread(i):
                v = mm(dband[d, at(i, tile), :], x[d, window(i, tile, span), :])
                t[d, at(i, tile), :] = (PRICE_STEP * v[:, :width]).astype(BF)
                if k < INNER_ITERS:
                    if isinstance(i, int):
                        padded = pl.ds(PAD + i * tile, tile)
                    else:
                        padded = pl.ds(pl.multiple_of(PAD + i * tile, PAD), tile)
                    half_v = v[:, low:]
                    old = exc[d, padded, :].astype(F32)
                    exc[d, padded, :] = (old + ext_of(half_v, k)).astype(BF)
                    off[d, padded, :] = half_v

            each(blocks, spread)

        for d in range(districts):
            def advance(i):
                if isinstance(i, int):
                    padded = pl.ds(PAD + i * tile, tile)
                else:
                    padded = pl.ds(pl.multiple_of(PAD + i * tile, PAD), tile)
                f = f0[d, at(i, tile), :] - mm(t[d, at(i, tile), :], m_ref[d])
                new = h[d, at(i, tile), :] + f
                h[d, at(i, tile), :] = new
                x[d, padded, :width] = new.astype(BF)
                if k < INNER_ITERS - 1:
                    x[d, padded, width:] = off[d, padded, :][:, width - low:].astype(BF)
                if k == INNER_ITERS - 1 or k == steps - 1:
                    fl[d, at(i, tile), :] = f.astype(BF)

            each(blocks, advance)

        if k == INNER_ITERS - 1 or k == steps - 1:
            target = d0_ref if k == INNER_ITERS - 1 else d1_ref
            draws = jnp.zeros((RESERVOIRS, LANES), F32)
            for d in range(districts):
                draws += mm_tn(exc[d, PAD:PAD + count, :], fl[d, :, :LANES])[:RESERVOIRS]
            target[...] = draws

    per = LANES // rows
    for d in range(districts):
        own_rel = relown_ref[d:d + 1, 0:rows]
        for q in range(1, per):
            own_rel = jnp.where(my % per == q, relown_ref[d:d + 1, q * rows:(q + 1) * rows], own_rel)
        hot = (iota((count, rows), 0) == own_rel).astype(F32).astype(BF)
        tb_ref[d] = mm_tn(hot, t[d])
        qg_ref[d] = mm_tn(hot, exc[d, PAD:PAD + count, :]).astype(BF)
        start = pl.multiple_of(my * rows, rows)
        own_off = (g_ref[my, d])[:, low:].astype(F32)
        own_band = band(own_off, rows, rows + 2 * PAD, PAD, width - low).astype(BF)
        pb_ref[d] = PRICE_STEP * mm(own_band, x[d, pl.ds(start, rows + 2 * PAD), :])[:, :width]
        ql_ref[d] = mm(own_band, exc[d, pl.ds(start, rows + 2 * PAD), :]).astype(BF)
        gm_ref[d] = mm_tn(exc[d, PAD:PAD + count, :], exc[d, PAD:PAD + count, :])[:RESERVOIRS].astype(BF)
        power = (iota((horizon, width), 0) == iota((horizon, width), 1)).astype(F32).astype(BF)
        mp_ref[d, 0] = power
        for j in range(INNER_ITERS):
            power = mm(power, m_ref[d]).astype(BF)
            mp_ref[d, j + 1] = power


def finish_body(dr_ref, cap_ref, d1_ref, pb_ref, tb_ref, ql_ref, qg_ref, gm_ref, mp_ref, y_ref, z_ref,
                plan_ref, price_ref, dual_ref, draw_ref, *, scale, horizon):
    districts = pb_ref.shape[0]
    drawn = dr_ref[0]
    for q in range(1, dr_ref.shape[0]):
        drawn = drawn + dr_ref[q]
    duals = (drawn[:, :horizon] - cap_ref[...]) * scale
    dual_ref[...] = duals
    high = duals.astype(BF)
    both = jnp.concatenate([duals, duals - high.astype(F32)], axis=0).astype(BF)
    n = INNER_ITERS
    draws = d1_ref[...]
    for d in range(districts):
        grown = []
        for j in range(n + 1):
            parts = mm(both, mp_ref[d, j])
            grown.append(parts[:RESERVOIRS] + parts[RESERVOIRS:])

        def stacked(first, weights):
            rows = [w * grown[first + j] for j, w in enumerate(weights)]
            filler = jnp.zeros((LANES - n * RESERVOIRS, rows[0].shape[1]), F32)
            whole = jnp.concatenate(rows + [filler], axis=0)
            top = whole.astype(BF)
            return top, (whole - top.astype(F32)).astype(BF)

        def apply(left, pair):
            return mm(left, pair[0]) + mm(left, pair[1])

        term = [math.comb(n - 1, j) * (-PRICE_STEP) ** j for j in range(n)]
        sums = [-PRICE_STEP * math.comb(n, j + 1) * (-PRICE_STEP) ** j for j in range(n)]
        prices = (tb_ref[d] + apply(qg_ref[d], stacked(0, term))).astype(BF)
        plan_ref[d] = -(y_ref[d] + mm(prices, z_ref[d]))
        price_ref[d] = pb_ref[d] + apply(ql_ref[d], stacked(1, sums))
        draws = draws - apply(gm_ref[d], stacked(1, term))[:, :LANES]
    draw_ref[...] = draws


def on_device(cost_terms, neighbours, relayout, ownership, capacity, coupling, solve_factor):
    districts, rows, unknowns = cost_terms.shape
    width = coupling.shape[2]
    horizon = capacity.shape[1]
    subs = lax.axis_size("sub")
    count = rows * subs
    assert relayout.shape[1] == count
    my = lax.axis_index("sub").astype(jnp.int32).reshape(1)
    chunk = 256
    chunks = unknowns // chunk
    total = width + 64
    owner_at = width + 16
    tile = LANES
    load_count = districts * lax.axis_size("district") * count // (2 * RESERVOIRS)
    scale = RESERVE_STEP / math.sqrt(load_count)
    limit = pltpu.CompilerParams(vmem_limit_bytes=56 * 1024 * 1024)

    y, z, m, payload = pl.pallas_call(
        functools.partial(prepare_body, rows=rows, width=width, chunk=chunk, owner_at=owner_at),
        grid_spec=pltpu.PrefetchScalarGridSpec(
            num_scalar_prefetch=1,
            grid=(districts, chunks),
            in_specs=[
                pl.BlockSpec((1, rows, unknowns), lambda d, j, s: (d, 0, 0)),
                pl.BlockSpec((1, unknowns, chunk), lambda d, j, s: (d, 0, j)),
                pl.BlockSpec((1, unknowns, width), lambda d, j, s: (d, 0, 0)),
                pl.BlockSpec((1, rows, LINK_COUNT), lambda d, j, s: (d, 0, 0)),
                pl.BlockSpec((districts, rows), lambda d, j, s: (0, 0)),
            ],
            out_specs=[
                pl.BlockSpec((1, rows, chunk), lambda d, j, s: (d, 0, j)),
                pl.BlockSpec((1, width, chunk), lambda d, j, s: (d, 0, j)),
                pl.BlockSpec((1, width, width), lambda d, j, s: (d, 0, 0)),
                pl.BlockSpec((1, rows, total), lambda d, j, s: (d, 0, 0)),
            ],
            scratch_shapes=[
                pltpu.VMEM((rows + width, unknowns), BF),
                pltpu.VMEM((rows + width, width), F32),
            ],
        ),
        out_shape=[
            jax.ShapeDtypeStruct((districts, rows, unknowns), F32),
            jax.ShapeDtypeStruct((districts, width, unknowns), BF),
            jax.ShapeDtypeStruct((districts, width, width), BF),
            jax.ShapeDtypeStruct((districts, rows, total), BF),
        ],
        compiler_params=limit,
        name="prepare",
    )(my, cost_terms, solve_factor, coupling, neighbours, ownership)

    gathered = lax.all_gather(payload, "sub", axis=0, tiled=False)

    whole = lambda shape: pl.BlockSpec(shape, lambda i, s: (0,) * len(shape))
    per = LANES // rows
    out_shapes = [
        ((RESERVOIRS, LANES), F32),
        ((RESERVOIRS, LANES), F32),
        ((districts, rows, width), F32),
        ((districts, rows, width), F32),
        ((districts, rows, LANES), BF),
        ((districts, rows, LANES), BF),
        ((districts, RESERVOIRS, LANES), BF),
        ((districts, INNER_ITERS + 1, horizon, width), BF),
    ]
    d0, d1, pb, tb, ql, qg, gm, mp = pl.pallas_call(
        functools.partial(
            iterate_body, rows=rows, width=width, horizon=horizon, tile=tile, owner_at=owner_at
        ),
        grid_spec=pltpu.PrefetchScalarGridSpec(
            num_scalar_prefetch=1,
            grid=(1,),
            in_specs=[
                whole((subs, districts, rows, total)),
                whole((districts, count)),
                pl.BlockSpec((districts, LANES), lambda i, s: (0, s[0] // per)),
                whole((districts, width, width)),
            ],
            out_specs=[whole(shape) for shape, _ in out_shapes],
            scratch_shapes=[
                pltpu.VMEM((districts, count + 2 * PAD, LANES), F32),
                pltpu.VMEM((districts, count, tile + 2 * PAD), BF),
                pltpu.VMEM((districts, count + 2 * PAD, total), BF),
                pltpu.VMEM((districts, count, width), F32),
                pltpu.VMEM((districts, count, width), F32),
                pltpu.VMEM((districts, count, width), BF),
                pltpu.VMEM((districts, count + 2 * PAD, LANES), BF),
                pltpu.VMEM((districts, count, width), BF),
            ],
        ),
        out_shape=[jax.ShapeDtypeStruct(shape, kind) for shape, kind in out_shapes],
        compiler_params=limit,
        name="iterate",
    )(my, gathered, relayout, relayout, m)

    drawn = lax.all_gather(d0, "district", axis=0, tiled=False)

    plan, prices, duals, draws = pl.pallas_call(
        functools.partial(finish_body, scale=scale, horizon=horizon),
        out_shape=[
            jax.ShapeDtypeStruct((districts, rows, unknowns), F32),
            jax.ShapeDtypeStruct((districts, rows, width), F32),
            jax.ShapeDtypeStruct((RESERVOIRS, horizon), F32),
            jax.ShapeDtypeStruct((RESERVOIRS, LANES), F32),
        ],
        compiler_params=limit,
        name="finish",
    )(drawn, capacity, d1, pb, tb, ql, qg, gm, mp, y, z)

    drawn = lax.all_gather(draws, "district", axis=0, tiled=False)
    total_draws = jnp.sum(drawn, axis=0)[:, :horizon]
    duals = duals + (total_draws - capacity) * scale
    return plan, prices, duals


def solution(mesh):
    placed = (
        P("district", "sub", None),
        P("district", "sub", None),
        P("district", None),
        P("district", "sub"),
        P(),
        P("district", None, None),
        P("district", None, None),
    )
    return jax.shard_map(
        on_device,
        mesh=mesh,
        in_specs=placed,
        out_specs=(P("district", "sub", None), P("district", "sub", None), P()),
        check_vma=False,
    )
```

```python
import functools
import math

import jax
import jax.numpy as jnp
from jax import lax
from jax.experimental import pallas as pl
from jax.experimental.pallas import tpu as pltpu
from jax.sharding import PartitionSpec as P

REACH_SPAN = 16
LINK_COUNT = 4
RESERVOIRS = 16
OUTER_ITERS = 2
INNER_ITERS = 4

PRICE_STEP = 0.3
RESERVE_STEP = 1.0

LANES = 128
PAD = 2 * REACH_SPAN

BF = jnp.bfloat16
F32 = jnp.float32


def mm(a, b):
    return jnp.dot(a, b, preferred_element_type=F32)


def mm_nt(a, b):
    return lax.dot_general(a, b, (((1,), (1,)), ((), ())), preferred_element_type=F32)


def mm_tn(a, b):
    return lax.dot_general(a, b, (((0,), (0,)), ((), ())), preferred_element_type=F32)


def iota(shape, dim):
    return lax.broadcasted_iota(jnp.int32, shape, dim)


def each(count, step):
    if count <= 8:
        for i in range(count):
            step(i)
    else:
        lax.fori_loop(0, count, lambda i, c: (step(i), c)[1], 0)


def at(i, size):
    if isinstance(i, int):
        return pl.ds(i * size, size)
    return pl.ds(pl.multiple_of(i * size, size), size)


def window(i, size, width):
    if isinstance(i, int):
        return pl.ds(i * size, width)
    return pl.ds(pl.multiple_of(i * size, size), width)


def gather_blocks(block, axis):
    n = lax.axis_size(axis)
    if n > 8 or n % 2:
        return [lax.all_gather(block, axis, axis=0, tiled=False)]
    other = lax.ppermute(block, axis, [(i, i ^ 1) for i in range(n)])
    pair = jnp.stack([block, other])
    turned = [
        lax.ppermute(pair, axis, [(i, (i + 2 * k) % n) for i in range(n)]) for k in range(1, n // 2)
    ]
    return [pair] + turned


def origins(my, n, arrays):
    if arrays == 1:
        return [[s for s in range(n)]]
    out = []
    for k in range(arrays):
        source = lax.rem(my + n - 2 * k, n)
        swapped = source + 1 - 2 * lax.rem(source, 2)
        out.append([source, swapped])
    return out


def gather_few(block, axis):
    n = lax.axis_size(axis)
    if n & (n - 1):
        whole = lax.all_gather(block, axis, axis=0, tiled=False)
        return [whole[i] for i in range(n)]
    return [block] + [lax.ppermute(block, axis, [(i, i ^ k) for i in range(n)]) for k in range(1, n)]


def tree(parts):
    while len(parts) > 1:
        last = [parts[-1]] if len(parts) % 2 else []
        parts = [parts[i] + parts[i + 1] for i in range(0, len(parts) - 1, 2)] + last
    return parts[0]


def prepare_body(my_ref, cost_ref, s_ref, c_ref, nb_ref, own_ref, y_ref, z_ref, m_ref, pay_ref,
                 lhs, acc, *, rows, width, chunk, owner_at):
    d = pl.program_id(0)
    j = pl.program_id(1)

    @pl.when(j == 0)
    def _():
        lhs[:rows, :] = cost_ref[0]
        lhs[rows:, :] = c_ref[0]
        acc[...] = jnp.zeros_like(acc)

    yz = mm(lhs[...], s_ref[0])
    y_ref[0] = yz[:rows]
    yzb = yz.astype(BF)
    z_ref[0] = yzb[rows:]
    acc[...] += mm_nt(yzb, c_ref[0, :, pl.ds(pl.multiple_of(j * chunk, chunk), chunk)])

    @pl.when(j == pl.num_programs(1) - 1)
    def _():
        pay_ref[0, :, 0:width] = (-acc[:rows]).astype(BF)
        m_ref[0] = acc[rows:].astype(BF)
        total = pay_ref.shape[2]
        own = own_ref[pl.ds(d, 1), :]
        slot = iota((total, rows), 0) - owner_at
        hot = ((slot == own) & (slot >= 0) & (slot < RESERVOIRS)).astype(F32)
        eye = (iota((rows, rows), 0) == iota((rows, rows), 1)).astype(F32)
        off = (nb_ref[0] - my_ref[0] * rows - iota((LINK_COUNT, rows), 1)).astype(F32)
        line = iota((total, rows), 0)
        for k in range(LINK_COUNT):
            hot = jnp.where(line == width + k, off[k:k + 1, :], hot)
        ext = mm_nt(eye.astype(BF), hot.astype(BF))
        pay_ref[0, :, width:] = ext[:, width:].astype(BF)


def band(off, rows, columns, shift, first_lane):
    column = iota((rows, columns), 1) - iota((rows, columns), 0) - shift
    out = (column == 0).astype(F32)
    for k in range(LINK_COUNT):
        offset = off[:, first_lane + k:first_lane + k + 1].astype(jnp.int32)
        out = out - jnp.where(column == offset, 1.0 / LINK_COUNT, 0.0)
    return out


def iterate_body(my_ref, *refs, arrays, subs, rows, width, horizon, tile, owner_at):
    g_refs = refs[:arrays]
    rel_ref, relown_ref, m_ref = refs[arrays:arrays + 3]
    msg_ref, pb_ref, tb_ref, ql_ref, qg_ref, mp_ref = refs[arrays + 3:arrays + 9]
    off, dband, x, h, f0, t, exc, fl = refs[arrays + 9:]
    districts = g_refs[0].shape[1]
    total = g_refs[0].shape[3]
    count = rows * subs
    blocks = count // tile
    low = total - LANES
    span = tile + 2 * PAD
    my = my_ref[0]
    half = iota((tile, LANES), 1)
    own_lane = owner_at - low

    def ext_of(v, power):
        moved = pltpu.roll(v, (power * RESERVOIRS - own_lane) % LANES, 1)
        keep = (half >= power * RESERVOIRS) & (half < (power + 1) * RESERVOIRS)
        return jnp.where(keep, moved, 0.0)

    for d in range(districts):
        off[d, :PAD, :] = jnp.zeros((PAD, LANES), F32)
        off[d, PAD + count:, :] = jnp.zeros((PAD, LANES), F32)
        x[d, :PAD, :] = jnp.zeros((PAD, total), BF)
        x[d, PAD + count:, :] = jnp.zeros((PAD, total), BF)
        exc[d, :PAD, :] = jnp.zeros((PAD, LANES), BF)
        exc[d, PAD + count:, :] = jnp.zeros((PAD, LANES), BF)

        def unpack(s, block):
            here = at(s, rows)
            if isinstance(s, int):
                padded = pl.ds(PAD + s * rows, rows)
            else:
                padded = pl.ds(pl.multiple_of(PAD + s * rows, PAD), rows)
            t[d, here, :] = block[:, :width]
            off[d, padded, :] = block[:, low:].astype(F32)
            x[d, padded, :] = block

        if arrays == 1:
            each(subs, lambda s: unpack(s, g_refs[0][s, d]))
        else:
            for g_ref, sources in zip(g_refs, origins(my, subs, arrays)):
                for b, s in enumerate(sources):
                    unpack(s, g_ref[b, d])

        def order(i):
            place = iota((tile, count), 0) + i * tile
            hot = (place == rel_ref[d:d + 1, :]).astype(F32).astype(BF)
            f0[d, at(i, tile), :] = mm(hot, t[d])

        each(blocks, order)

        def bands(i):
            full = band(off[d, window(i, tile, span), :], span, span, 0, width - low).astype(BF)
            dband[d, at(i, tile), :] = mm(full[PAD:PAD + tile], full).astype(BF)
            if isinstance(i, int):
                padded = pl.ds(PAD + i * tile, tile)
            else:
                padded = pl.ds(pl.multiple_of(PAD + i * tile, PAD), tile)
            f = f0[d, at(i, tile), :]
            h[d, at(i, tile), :] = f
            x[d, padded, :width] = f.astype(BF)
            exc[d, padded, :] = ext_of(off[d, padded, :], 0).astype(BF)

        each(blocks, bands)

    steps = OUTER_ITERS * INNER_ITERS
    for k in range(1, steps):
        for d in range(districts):
            def spread(i):
                v = mm(dband[d, at(i, tile), :], x[d, window(i, tile, span), :])
                t[d, at(i, tile), :] = (PRICE_STEP * v[:, :width]).astype(BF)
                if k < INNER_ITERS:
                    if isinstance(i, int):
                        padded = pl.ds(PAD + i * tile, tile)
                    else:
                        padded = pl.ds(pl.multiple_of(PAD + i * tile, PAD), tile)
                    half_v = v[:, low:]
                    old = exc[d, padded, :].astype(F32)
                    exc[d, padded, :] = (old + ext_of(half_v, k)).astype(BF)
                    off[d, padded, :] = half_v

            each(blocks, spread)

        for d in range(districts):
            def advance(i):
                if isinstance(i, int):
                    padded = pl.ds(PAD + i * tile, tile)
                else:
                    padded = pl.ds(pl.multiple_of(PAD + i * tile, PAD), tile)
                f = f0[d, at(i, tile), :] - mm(t[d, at(i, tile), :], m_ref[d])
                new = h[d, at(i, tile), :] + f
                h[d, at(i, tile), :] = new
                x[d, padded, :width] = new.astype(BF)
                if k < INNER_ITERS - 1:
                    x[d, padded, width:] = off[d, padded, :][:, width - low:].astype(BF)
                if k == INNER_ITERS - 1 or k == steps - 1:
                    fl[d, at(i, tile), :] = f.astype(BF)

            each(blocks, advance)

        if k == INNER_ITERS - 1 or k == steps - 1:
            first = 0 if k == INNER_ITERS - 1 else 2 * RESERVOIRS
            draws = jnp.zeros((RESERVOIRS, LANES), F32)
            for d in range(districts):
                draws += mm_tn(exc[d, PAD:PAD + count, :], fl[d, :, :LANES])[:RESERVOIRS]
            top = draws.astype(BF)
            msg_ref[first:first + RESERVOIRS, :] = top
            msg_ref[first + RESERVOIRS:first + 2 * RESERVOIRS, :] = (draws - top.astype(F32)).astype(BF)

    per = LANES // rows
    for d in range(districts):
        own_rel = relown_ref[d:d + 1, 0:rows]
        for q in range(1, per):
            own_rel = jnp.where(my % per == q, relown_ref[d:d + 1, q * rows:(q + 1) * rows], own_rel)
        hot = (iota((count, rows), 0) == own_rel).astype(F32).astype(BF)
        tb_ref[d] = mm_tn(hot, t[d])
        qg_ref[d] = mm_tn(hot, exc[d, PAD:PAD + count, :]).astype(BF)
        start = pl.multiple_of(my * rows, rows)
        own_off = (g_refs[0][my if arrays == 1 else 0, d])[:, low:].astype(F32)
        own_band = band(own_off, rows, rows + 2 * PAD, PAD, width - low).astype(BF)
        pb_ref[d] = PRICE_STEP * mm(own_band, x[d, pl.ds(start, rows + 2 * PAD), :])[:, :width]
        ql_ref[d] = mm(own_band, exc[d, pl.ds(start, rows + 2 * PAD), :]).astype(BF)
        start = 4 * RESERVOIRS + d * (RESERVOIRS + INNER_ITERS * horizon)
        response = mm_tn(exc[d, PAD:PAD + count, :], exc[d, PAD:PAD + count, :])[:RESERVOIRS]
        msg_ref[start:start + RESERVOIRS, :] = response.astype(BF)
        start += RESERVOIRS
        power = (iota((horizon, width), 0) == iota((horizon, width), 1)).astype(F32).astype(BF)
        mp_ref[d, 0] = power
        for j in range(INNER_ITERS):
            power = mm(power, m_ref[d]).astype(BF)
            mp_ref[d, j + 1] = power
            msg_ref[start + j * horizon:start + (j + 1) * horizon, :] = power[:, :LANES]


def finish_body(*refs, pieces, scale, horizon):
    msgs = refs[:pieces]
    cap_ref, pb_ref, tb_ref, ql_ref, qg_ref, mp_ref, y_ref, z_ref = refs[pieces:pieces + 8]
    plan_ref, price_ref, dual_ref = refs[pieces + 8:]
    districts = pb_ref.shape[0]
    n = INNER_ITERS

    def drawn(first):
        sums = []
        for msg in msgs:
            high = msg[first:first + RESERVOIRS, :].astype(F32)
            sums.append(high + msg[first + RESERVOIRS:first + 2 * RESERVOIRS, :].astype(F32))
        return sums

    duals = (tree(drawn(0))[:, :horizon] - cap_ref[...]) * scale
    high = duals.astype(BF)
    both = jnp.concatenate([duals, duals - high.astype(F32)], axis=0).astype(BF)
    term = [math.comb(n - 1, j) * (-PRICE_STEP) ** j for j in range(n)]
    sums = [-PRICE_STEP * math.comb(n, j + 1) * (-PRICE_STEP) ** j for j in range(n)]

    def grow(power):
        parts = mm(both, power)
        return parts[:RESERVOIRS] + parts[RESERVOIRS:]

    def stacked(grown, weights):
        rows = [w * g for g, w in zip(grown, weights)]
        filler = jnp.zeros((LANES - n * RESERVOIRS, rows[0].shape[1]), F32)
        return jnp.concatenate(rows + [filler], axis=0)

    def apply(left, whole):
        top = whole.astype(BF)
        return mm(left, top) + mm(left, (whole - top.astype(F32)).astype(BF))

    for d in range(districts):
        grown = [grow(mp_ref[d, j]) for j in range(n + 1)]
        prices = (tb_ref[d] + apply(qg_ref[d], stacked(grown, term))).astype(BF)
        plan_ref[d] = -(y_ref[d] + mm(prices, z_ref[d]))
        price_ref[d] = pb_ref[d] + apply(ql_ref[d], stacked(grown[1:], sums))

    draws = []
    for msg, value in zip(msgs, drawn(2 * RESERVOIRS)):
        for d in range(districts):
            start = 4 * RESERVOIRS + d * (RESERVOIRS + n * horizon)
            response = msg[start:start + RESERVOIRS, :]
            start += RESERVOIRS
            grown = [grow(msg[start + j * horizon:start + (j + 1) * horizon, :]) for j in range(n)]
            value = value - apply(response, stacked(grown, term))
        draws.append(value)
    dual_ref[...] = duals + (tree(draws)[:, :horizon] - cap_ref[...]) * scale


def on_device(cost_terms, neighbours, relayout, ownership, capacity, coupling, solve_factor):
    districts, rows, unknowns = cost_terms.shape
    width = coupling.shape[2]
    horizon = capacity.shape[1]
    subs = lax.axis_size("sub")
    count = rows * subs
    assert relayout.shape[1] == count
    my = lax.axis_index("sub").astype(jnp.int32).reshape(1)
    chunk = 256
    chunks = unknowns // chunk
    total = width + 64
    owner_at = width + 16
    tile = LANES
    load_count = districts * lax.axis_size("district") * count // (2 * RESERVOIRS)
    scale = RESERVE_STEP / math.sqrt(load_count)
    limit = pltpu.CompilerParams(vmem_limit_bytes=56 * 1024 * 1024)

    y, z, m, payload = pl.pallas_call(
        functools.partial(prepare_body, rows=rows, width=width, chunk=chunk, owner_at=owner_at),
        grid_spec=pltpu.PrefetchScalarGridSpec(
            num_scalar_prefetch=1,
            grid=(districts, chunks),
            in_specs=[
                pl.BlockSpec((1, rows, unknowns), lambda d, j, s: (d, 0, 0)),
                pl.BlockSpec((1, unknowns, chunk), lambda d, j, s: (d, 0, j)),
                pl.BlockSpec((1, width, unknowns), lambda d, j, s: (d, 0, 0)),
                pl.BlockSpec((1, LINK_COUNT, rows), lambda d, j, s: (d, 0, 0)),
                pl.BlockSpec((districts, rows), lambda d, j, s: (0, 0)),
            ],
            out_specs=[
                pl.BlockSpec((1, rows, chunk), lambda d, j, s: (d, 0, j)),
                pl.BlockSpec((1, width, chunk), lambda d, j, s: (d, 0, j)),
                pl.BlockSpec((1, width, width), lambda d, j, s: (d, 0, 0)),
                pl.BlockSpec((1, rows, total), lambda d, j, s: (d, 0, 0)),
            ],
            scratch_shapes=[
                pltpu.VMEM((rows + width, unknowns), BF),
                pltpu.VMEM((rows + width, width), F32),
            ],
        ),
        out_shape=[
            jax.ShapeDtypeStruct((districts, rows, unknowns), F32),
            jax.ShapeDtypeStruct((districts, width, unknowns), BF),
            jax.ShapeDtypeStruct((districts, width, width), BF),
            jax.ShapeDtypeStruct((districts, rows, total), BF),
        ],
        compiler_params=limit,
        name="prepare",
    )(my, cost_terms, solve_factor, coupling.swapaxes(1, 2), neighbours.swapaxes(1, 2), ownership)

    gathered = gather_blocks(payload, "sub")

    whole = lambda shape: pl.BlockSpec(shape, lambda i, s: (0,) * len(shape))
    per = LANES // rows
    message = 4 * RESERVOIRS + districts * (RESERVOIRS + INNER_ITERS * horizon)
    out_shapes = [
        ((message, LANES), BF),
        ((districts, rows, width), F32),
        ((districts, rows, width), F32),
        ((districts, rows, LANES), BF),
        ((districts, rows, LANES), BF),
        ((districts, INNER_ITERS + 1, horizon, width), BF),
    ]
    sent, pb, tb, ql, qg, mp = pl.pallas_call(
        functools.partial(
            iterate_body, arrays=len(gathered), subs=subs, rows=rows, width=width, horizon=horizon, tile=tile, owner_at=owner_at
        ),
        grid_spec=pltpu.PrefetchScalarGridSpec(
            num_scalar_prefetch=1,
            grid=(1,),
            in_specs=[
                *[whole(piece.shape) for piece in gathered],
                whole((districts, count)),
                pl.BlockSpec((districts, LANES), lambda i, s: (0, s[0] // per)),
                whole((districts, width, width)),
            ],
            out_specs=[whole(shape) for shape, _ in out_shapes],
            scratch_shapes=[
                pltpu.VMEM((districts, count + 2 * PAD, LANES), F32),
                pltpu.VMEM((districts, count, tile + 2 * PAD), BF),
                pltpu.VMEM((districts, count + 2 * PAD, total), BF),
                pltpu.VMEM((districts, count, width), F32),
                pltpu.VMEM((districts, count, width), F32),
                pltpu.VMEM((districts, count, width), BF),
                pltpu.VMEM((districts, count + 2 * PAD, LANES), BF),
                pltpu.VMEM((districts, count, width), BF),
            ],
        ),
        out_shape=[jax.ShapeDtypeStruct(shape, kind) for shape, kind in out_shapes],
        compiler_params=limit,
        name="iterate",
    )(my, *gathered, relayout, relayout, m)

    received = gather_few(sent, "district")

    plan, prices, duals = pl.pallas_call(
        functools.partial(finish_body, pieces=len(received), scale=scale, horizon=horizon),
        out_shape=[
            jax.ShapeDtypeStruct((districts, rows, unknowns), F32),
            jax.ShapeDtypeStruct((districts, rows, width), F32),
            jax.ShapeDtypeStruct((RESERVOIRS, horizon), F32),
        ],
        compiler_params=limit,
        name="finish",
    )(*received, capacity, pb, tb, ql, qg, mp, y, z)
    return plan, prices, duals


def solution(mesh):
    placed = (
        P("district", "sub", None),
        P("district", "sub", None),
        P("district", None),
        P("district", "sub"),
        P(),
        P("district", None, None),
        P("district", None, None),
    )
    return jax.shard_map(
        on_device,
        mesh=mesh,
        in_specs=placed,
        out_specs=(P("district", "sub", None), P("district", "sub", None), P()),
        check_vma=False,
    )
```
